128 devices in a mesh: row: 16 (over y, x_hi, core), tensor: 8 (over x_lo, z).
Axes of the slice: x: 4 (x_hi: 2, x_lo: 2; x = x_hi * 2 + x_lo), y: 4, z: 4, core: 2. Of those that a mesh axis runs over, the one named last changes fastest.
Arguments:
- hidden_rows: bfloat16 [4096, 8192], P('row'), may hold values from -6 to 6
- w_query: bfloat16 [8192, 8192], P('row', 'tensor'), may hold values from -0.0625 to 0.0625
- w_out: bfloat16 [8192, 8192], P('tensor', 'row'), may hold values from -0.0625 to 0.0625
- pack_key_cache: bfloat16 [131072, 1024], P('row', 'tensor'), may hold values from -250 to 250
- pack_value_cache: bfloat16 [131072, 1024], P('row', 'tensor'), may hold values from -6 to 6
- query_pos: int32 [4096], P('row'), may hold values from 0 to 131071, as said below
- doc_blocks: int32 [16, 4], P('row'), may hold values from 1 to 32, 64 in all within a row
Outputs:
- mixed: bfloat16 [4096, 8192], P('row', 'tensor')
The draws below stay inside these ranges and needn't reach their ends.
Inputs may be any that keep to these rules, and one draw needn't show every extreme that they name: `query_pos`: each index of row holds 256 consecutive query rows; at most 32 of them lie in any one block of 8192 key positions, and exactly 32 in some blocks. Positions may repeat. `doc_blocks`: each row sums to 64.
All inputs are finite; a program needn't handle non-finite values.
Results may differ from the reference program's by a relative error of at most 0.014.
The reference program's roundings to bfloat16 on the way count: a program that leaves them out, or rounds other values in their place, can miss the bound.
Values may be sent and summed in bfloat16 or wider, within the bound.
No kernel may reach another device: no remote copies, remote signals or barrier semaphores. Data moves between devices by JAX's collectives and lax.ppermute only.
A program may use at most 128 MiB of HBM per device.

```python
import math
import jax
import jax.numpy as jnp
import numpy as np
from jax import lax

D = 8192
QUERY_HEADS = 64
KEY_VALUE_HEADS = 8
HEAD_SIZE = 128
QRY_DEV = 256
KEY_DEV = 8192
DOCS = 4
QROWS = 4096
KEY_POSITIONS = 131072
N_ROW = 16
N_TENSOR = 8


def draw_query_pos(key, part):
    capacity = 2 * QRY_DEV // N_ROW
    rank_key, noise_key, perm_key, offset_key = jax.random.split(key, 4)
    global_rank = jax.random.permutation(rank_key, N_ROW).astype(jnp.int32)
    noise = jax.random.randint(noise_key, (N_ROW, N_ROW), 0, 2 * N_ROW).astype(jnp.int32)
    server_ids = jnp.arange(N_ROW, dtype=jnp.int32)
    ranking = (global_rank[None, :] + noise) * N_ROW + server_ids[None, :]
    order = jnp.argsort(ranking, axis=1, stable=True).astype(jnp.int32)
    levels = jnp.where(server_ids < N_ROW // 4, capacity, jnp.where(server_ids < N_ROW // 2, capacity // 2, capacity // 4)).astype(jnp.int32)
    counts = jnp.zeros((N_ROW, N_ROW), jnp.int32).at[server_ids[:, None], order].set(jnp.broadcast_to(levels[None, :], (N_ROW, N_ROW)))

    def one_source(count_row, source_key):
        listed = jnp.repeat(server_ids, count_row, total_repeat_length=QRY_DEV)
        return jax.random.permutation(source_key, listed)
    source_keys = jax.random.split(perm_key, N_ROW)
    target_server = jax.vmap(one_source)(counts, source_keys)
    offsets = jax.random.randint(offset_key, (N_ROW, QRY_DEV), 0, KEY_DEV).astype(jnp.int32)
    return (target_server * KEY_DEV + offsets).reshape(QROWS).astype(jnp.int32)


def draw_pack_key_cache(key, part):
    base_key = jax.random.fold_in(jax.random.fold_in(key, 7), 0)
    array_shape = (KEY_POSITIONS, KEY_VALUE_HEADS * HEAD_SIZE)
    base = jax.random.normal(base_key, array_shape, jnp.float32)
    return jnp.clip(base, -6.0, 6.0).astype(jnp.bfloat16)


def block_levels(own_key, shape, cuts, least, largest):
    level, own = 1.0, jax.random.fold_in(own_key, 6)
    for axis_at, parts in cuts:
        heights = jnp.exp(jax.random.uniform(jax.random.fold_in(own, axis_at), (parts,), jnp.float32, least / len(cuts), largest / len(cuts)))
        level = level * jnp.repeat(heights, shape[axis_at] // parts).reshape([-1 if axis == axis_at else 1 for axis in range(len(shape))])
    return level


def length_profile(amount, total, reach, slope):
    weights = [(1 << 20) // math.isqrt(standing ** slope) + 1 for standing in range(2, amount + 1)]
    surplus, given = total - reach - (amount - 1), [1] * (amount - 1)
    while surplus > 0:
        free = [i for i in range(amount - 1) if given[i] < reach]
        whole, remaining = sum([weights[i] for i in free]), surplus
        for i in free:
            extra = min(reach - given[i], max(1, remaining * weights[i] // whole), surplus)
            given[i] = given[i] + extra
            surplus = surplus - extra
    return np.array([reach] + given)


def uneven(key, amount, total, bound, skew):
    if amount == 2:
        one = jax.random.randint(key, (), max(1, total - bound), min(bound, total - 1) + 1)
        return jnp.stack([one, total - one])
    sizes = jnp.asarray(length_profile(amount, total, bound, skew), jnp.int32)
    couples = (amount - 1) // 2
    source_of, receiver = sizes[1:1 + 2 * couples:2], sizes[2:2 + 2 * couples:2]
    room = jnp.minimum(source_of - 1, bound - receiver)
    shifted = jax.random.randint(jax.random.fold_in(key, 1), (couples,), 0, 1 << 20) % (room + 1)
    sizes = sizes.at[1:1 + 2 * couples:2].set(source_of - shifted).at[2:2 + 2 * couples:2].set(receiver + shifted)
    return sizes[jax.random.permutation(jax.random.fold_in(key, 2), amount)]


def bell_draw(stream_key, extent, spread, limit, cuts=(), kind=jnp.bfloat16):
    drawn = spread * jax.random.normal(stream_key, extent, jnp.float32)
    if cuts:
        drawn = drawn * block_levels(stream_key, extent, cuts, -0.22, 0.18)
    return jnp.clip(drawn, -limit, limit).astype(kind)


def setup_inputs(seed: int = 0) -> dict:
    key_of = jax.random.split(jax.random.key(seed), 8)
    return {
        "hidden_rows": bell_draw(key_of[0], (QROWS, D), 1.0, 6.0, ((0, 16),)),
        "w_query": bell_draw(key_of[1], (D, QUERY_HEADS * HEAD_SIZE), D ** -0.5, 0.0625, ((0, 16), (1, 8))),
        "w_out": bell_draw(key_of[2], (QUERY_HEADS * HEAD_SIZE, D), (QUERY_HEADS * HEAD_SIZE) ** -0.5, 0.0625, ((0, 8), (1, 16))),
        "pack_key_cache": draw_pack_key_cache(jax.random.fold_in(key_of[7], 71), 0),
        "pack_value_cache": bell_draw(key_of[4], (KEY_POSITIONS, KEY_VALUE_HEADS * HEAD_SIZE), 1.0, 6.0, ((0, 16), (1, 8))),
        "query_pos": draw_query_pos(jax.random.fold_in(key_of[7], 71), 0),
        "doc_blocks": jax.vmap(lambda own: uneven(own, DOCS, KEY_DEV // 128, KEY_DEV // 256, 2))(jax.random.split(key_of[6], N_ROW)).reshape((N_ROW, DOCS)).astype(jnp.int32),
    }


neg_large = -1e+30

def attend_block(queries_blk, pos_blk, pack_key_cache, pack_value_cache, doc_blocks):
    window_length = KEY_DEV
    heads_per_group = QUERY_HEADS // KEY_VALUE_HEADS
    key_index = jnp.arange(window_length, dtype=jnp.int32)
    score_scale = 1.0 / math.sqrt(HEAD_SIZE)

    def single(single_query_row, position):
        server = (position // window_length).astype(jnp.int32)
        offset = position - server * window_length
        first_row_index = (server * window_length).astype(jnp.int32)
        picked_key_rows = lax.dynamic_slice_in_dim(pack_key_cache, first_row_index, window_length, 0).reshape(window_length, KEY_VALUE_HEADS, HEAD_SIZE)
        picked_value_rows = lax.dynamic_slice_in_dim(pack_value_cache, first_row_index, window_length, 0).reshape(window_length, KEY_VALUE_HEADS, HEAD_SIZE)
        doc_ends = jnp.cumsum(doc_blocks[server]) * 128
        key_doc = lax.optimization_barrier(jnp.sum((key_index[:, None] >= doc_ends[None, :]).astype(jnp.int32), axis=1))
        query_doc = jnp.sum((offset >= doc_ends).astype(jnp.int32))
        allowed = (key_index <= offset) & (key_doc == query_doc)
        head_count = single_query_row.reshape(KEY_VALUE_HEADS, heads_per_group, HEAD_SIZE).astype(jnp.float32)
        scores = jnp.einsum('agd,kad->agk', head_count, picked_key_rows.astype(jnp.float32)) * score_scale
        scores = jnp.where(allowed[None, None, :], scores, neg_large)
        top_score = lax.optimization_barrier(jnp.max(scores, axis=2, keepdims=True))
        weights = jnp.where(allowed[None, None, :], jnp.exp(scores - top_score), 0.0)
        sums = lax.optimization_barrier(jnp.sum(weights, axis=2, keepdims=True))
        rounded = weights.astype(jnp.bfloat16).astype(jnp.float32)
        mixed_heads = jnp.einsum('agk,kad->agd', rounded, picked_value_rows.astype(jnp.float32))
        return (mixed_heads / sums).astype(jnp.bfloat16).reshape(QUERY_HEADS * HEAD_SIZE)
    return jax.vmap(single)(queries_blk, pos_blk)

def reference(hidden_rows, w_query, w_out, pack_key_cache, pack_value_cache, query_pos, doc_blocks):
    queries = jnp.dot(hidden_rows, w_query, preferred_element_type=jnp.float32).astype(jnp.bfloat16)
    block_rows = 4
    count = QROWS // block_rows

    def per_block(packed):
        return attend_block(packed[0], packed[1], pack_key_cache, pack_value_cache, doc_blocks)
    attended = lax.map(per_block, (queries.reshape(count, block_rows, QUERY_HEADS * HEAD_SIZE), query_pos.reshape(count, block_rows)))
    attended = attended.reshape(QROWS, QUERY_HEADS * HEAD_SIZE)
    part_width = QUERY_HEADS * HEAD_SIZE // N_TENSOR
    running = jnp.zeros((QROWS, D), jnp.float32)
    for group_idx in range(N_TENSOR):
        lower = group_idx * part_width
        term = jnp.dot(attended[:, lower:lower + part_width], w_out[lower:lower + part_width], preferred_element_type=jnp.float32).astype(jnp.bfloat16)
        term = lax.optimization_barrier(term)
        running = running + term.astype(jnp.float32)
    return running.astype(jnp.bfloat16)
```

```python
import functools
import math

import jax
import jax.numpy as jnp
from jax import lax
from jax.experimental import pallas as pl
from jax.experimental.pallas import tpu as pltpu
from jax.sharding import PartitionSpec as P

HEAD_SIZE = 128
NEG = -1e30
TILE = 64
KB = 1024
CHAIN = 128
N_Y, N_XH, N_CORE = 4, 2, 2
N_XL, N_Z = 2, 4


def row_moves(to):
    at = lambda y, h, c: (y * N_XH + h) * N_CORE + c
    return [(at(y, h, c), at(*to(y, h, c))) for y in range(N_Y) for h in range(N_XH) for c in range(N_CORE)]


def tensor_moves(to):
    at = lambda xl, z: xl * N_Z + z
    return [(at(xl, z), at(*to(xl, z))) for xl in range(N_XL) for z in range(N_Z)]


Y_UP = row_moves(lambda y, h, c: ((y + 1) % N_Y, h, c))
Y_DOWN = row_moves(lambda y, h, c: ((y - 1) % N_Y, h, c))
H_FLIP = row_moves(lambda y, h, c: (y, 1 - h, c))
C_FLIP = row_moves(lambda y, h, c: (y, h, 1 - c))
Z_UP = tensor_moves(lambda xl, z: (xl, (z + 1) % N_Z))
Z_DOWN = tensor_moves(lambda xl, z: (xl, (z - 1) % N_Z))
XL_FLIP = tensor_moves(lambda xl, z: (1 - xl, z))


def over_row(x, moves):
    return lax.ppermute(x, "row", moves)


def over_tensor(x, moves):
    return lax.ppermute(x, "tensor", moves)


def row_pieces(own):
    half = own.shape[0] // 2
    other_core = over_row(own, C_FLIP)
    other_h = over_row(own, H_FLIP)
    up = over_row(own, Y_UP)
    down = over_row(own, Y_DOWN)
    up2 = over_row(up[:half], Y_UP)
    down2 = over_row(down[half:], Y_DOWN)
    h_up_a = over_row(up[:half], H_FLIP)
    h_up_b = over_row(up[half:], H_FLIP)
    h_down = over_row(other_h, Y_DOWN)
    h_up2_a = over_row(h_up_a, Y_UP)
    h_up2_b = over_row(h_up_b, Y_UP)
    arrived = [
        (other_h, 0, 1, 0),
        (up, -1, 0, 0),
        (down, 1, 0, 0),
        (up2, -2, 0, 0),
        (down2, 2, 0, half),
        (h_up_a, -1, 1, 0),
        (h_up_b, -1, 1, half),
        (h_down, 1, 1, 0),
        (h_up2_a, -2, 1, 0),
        (h_up2_b, -2, 1, half),
    ]
    pieces = [(own, (0, 0, 0), 0), (other_core, (0, 0, 1), 0)]
    for piece, dy, dh, first in arrived:
        pieces.append((piece, (dy, dh, 0), first))
        pieces.append((over_row(piece, C_FLIP), (dy, dh, 1), first))
    return pieces


def member(row, shift):
    dy, dh, dc = shift
    y, h, c = row // (N_XH * N_CORE), (row // N_CORE) % N_XH, row % N_CORE
    return (((y + dy) % N_Y) * N_XH + (h ^ dh)) * N_CORE + (c ^ dc)


def attend_kernel(heads, bounds, perm, perm_t, q, offs, starts, k, vt, out, sorted_q, sorted_o, acc):
    tiles = offs.shape[0]
    lanes = heads * TILE
    chains = range(lanes // CHAIN)
    sorted_q[...] = jnp.dot(perm[...], q[...], preferred_element_type=jnp.float32).astype(jnp.bfloat16)
    sorted_o[...] = jnp.zeros_like(sorted_o)
    scale = math.log2(math.e) / math.sqrt(HEAD_SIZE)

    def tile(t, carry):
        lo, hi = bounds[0, t], bounds[1, t]

        @pl.when(hi > lo)
        def _():
            rows = pl.ds(pl.multiple_of(t * TILE, TILE), TILE)
            qt = jnp.concatenate([sorted_q[rows, pl.ds(h * HEAD_SIZE, HEAD_SIZE)] for h in range(heads)], axis=0)
            parts = [qt[c * CHAIN:(c + 1) * CHAIN] for c in chains]
            acc[...] = jnp.zeros_like(acc)

            def block(b, state):
                kb = k[pl.ds(pl.multiple_of(b * KB, KB), KB), :]
                key = b * KB + lax.broadcasted_iota(jnp.int32, (KB, CHAIN), 0)
                bias = jnp.where((key <= offs[t, :, :CHAIN]) & (key >= starts[t, :, :CHAIN]), 0.0, NEG)
                scores = [
                    lax.dot_general(kb, part, (((1,), (1,)), ((), ())), preferred_element_type=jnp.float32)
                    for part in parts
                ]
                new = []
                for c in chains:
                    top, total = state[c]
                    s = scores[c] * scale + bias
                    new_top = jnp.maximum(top, jnp.max(s, axis=0, keepdims=True))
                    p = jnp.exp2(s - new_top)
                    alpha = jnp.exp2(top - new_top)
                    cols = pl.ds(c * CHAIN, CHAIN)
                    acc[:, cols] = acc[:, cols] * alpha + jnp.dot(
                        vt[b], p.astype(jnp.bfloat16), preferred_element_type=jnp.float32
                    )
                    new.append((new_top, total * alpha + jnp.sum(p, axis=0, keepdims=True)))
                return tuple(new)

            init = tuple(
                (jnp.full((1, CHAIN), NEG, jnp.float32), jnp.zeros((1, CHAIN), jnp.float32)) for _ in chains
            )
            final = lax.fori_loop(lo, hi, block, init)
            total = jnp.concatenate([state[1] for state in final], axis=1)
            o = (acc[...] * (1.0 / total)).T.astype(jnp.bfloat16)
            for h in range(heads):
                sorted_o[rows, pl.ds(h * HEAD_SIZE, HEAD_SIZE)] = o[h * TILE:(h + 1) * TILE]

        return carry

    lax.fori_loop(0, tiles, tile, 0)
    out[...] = jnp.dot(perm_t[...], sorted_o[...], preferred_element_type=jnp.float32).astype(jnp.bfloat16)


def attend_tables(slot_offset, doc_lengths, heads):
    slots = slot_offset.shape[0]
    tiles = slots // TILE
    key = jnp.where(slot_offset < 0, 1 << 20, slot_offset)
    idx = jnp.arange(slots, dtype=jnp.int32)
    before = (key[None, :] < key[:, None]) | ((key[None, :] == key[:, None]) & (idx[None, :] < idx[:, None]))
    rank = jnp.sum(before.astype(jnp.int32), axis=1)
    perm = rank[None, :] == idx[:, None]
    perm_t = rank[:, None] == idx[None, :]
    offset = jnp.sum(jnp.where(perm, slot_offset[None, :], 0), axis=1)
    start, end = jnp.zeros_like(offset), 0
    for d in range(doc_lengths.shape[0]):
        end = end + doc_lengths[d] * 128
        start = jnp.where(offset >= end, end, start)
    tile_offset, tile_start = offset.reshape(tiles, TILE), start.reshape(tiles, TILE)
    top = jnp.max(tile_offset, axis=1)
    lo = jnp.where(top >= 0, tile_start[:, 0] // KB, 0)
    hi = jnp.where(top >= 0, top // KB + 1, 0)

    def spread(a):
        return jnp.broadcast_to(a[:, None, :], (tiles, heads, TILE)).reshape(tiles, 1, heads * TILE)

    return (
        jnp.stack([lo, hi]),
        perm.astype(jnp.bfloat16),
        perm_t.astype(jnp.bfloat16),
        spread(tile_offset),
        spread(tile_start),
    )


def attend(q, tables, k, vt):
    slots, width = q.shape
    heads = width // HEAD_SIZE
    bounds, perm, perm_t, offs, starts = tables
    vmem = pl.BlockSpec(memory_space=pltpu.VMEM)
    return pl.pallas_call(
        functools.partial(attend_kernel, heads),
        out_shape=jax.ShapeDtypeStruct((slots, width), jnp.bfloat16),
        in_specs=[pl.BlockSpec(memory_space=pltpu.SMEM)] + [vmem] * 7,
        out_specs=vmem,
        scratch_shapes=[
            pltpu.VMEM((slots, width), jnp.bfloat16),
            pltpu.VMEM((slots, width), jnp.bfloat16),
            pltpu.VMEM((HEAD_SIZE, heads * TILE), jnp.float32),
        ],
        name="attend",
    )(bounds, perm, perm_t, q, offs, starts, k, vt)


def exchange(x):
    return lax.all_to_all(x, "row", split_axis=0, concat_axis=0, tiled=True)


def added(a, b):
    return a.astype(jnp.float32) + b.astype(jnp.float32)


def rounded(a):
    return a.astype(jnp.bfloat16)


def reduce_z(part, z):
    half = part.shape[2] // 2
    at = lambda step: lax.dynamic_index_in_dim(part, (z + step) % N_Z, 1, keepdims=False)
    up1, down1, far, mine = at(1), at(3), at(2), at(0)
    far_up = over_tensor(far[:, :half], Z_UP)
    far_down = over_tensor(far[:, half:], Z_DOWN)
    up_b = over_tensor(up1[:, half:], Z_UP)
    down_a = over_tensor(down1[:, :half], Z_DOWN)
    up_a = over_tensor(rounded(added(up1[:, :half], far_up)), Z_UP)
    down_b = over_tensor(rounded(added(down1[:, half:], far_down)), Z_DOWN)
    top = added(mine[:, :half], down_a) + up_a.astype(jnp.float32)
    low = added(mine[:, half:], up_b) + down_b.astype(jnp.float32)
    return jnp.concatenate([top, low], axis=1)


def reduce_tensor(part):
    t = lax.axis_index("tensor")
    xl, z = t // N_Z, t % N_Z
    count, rows, cols = part.shape
    part = part.reshape(N_XL, N_Z, rows, cols)
    half = rows // 2
    first = reduce_z(part[:, :, :half], z)
    pick = lambda a, i: lax.dynamic_index_in_dim(a, i, 0, keepdims=False)
    first = rounded(added(pick(first, xl), over_tensor(rounded(pick(first, 1 - xl)), XL_FLIP)))
    second = part[:, :, half:]
    other = over_tensor(pick(second, 1 - xl), XL_FLIP)
    second = rounded(added(pick(second, xl), other))
    second = rounded(reduce_z(second[None], z)[0])
    return jnp.concatenate([first, second], axis=0)


def body(hidden_rows, w_query, w_out, pack_key_cache, pack_value_cache, query_pos, doc_blocks):
    servers = lax.axis_size("row")
    groups = lax.axis_size("tensor")
    me = lax.axis_index("row")
    row_count = hidden_rows.shape[0]
    key_span = pack_key_cache.shape[0]
    capacity = 2 * row_count // servers
    slot_count = servers * capacity
    depth, head_width = w_query.shape
    col_width = w_out.shape[1]
    heads = head_width // HEAD_SIZE

    server = query_pos // key_span
    idx = jnp.arange(row_count, dtype=jnp.int32)
    earlier = (server[None, :] == server[:, None]) & (idx[None, :] < idx[:, None])
    slot = server * capacity + jnp.sum(earlier.astype(jnp.int32), axis=1)
    in_slot = jnp.arange(slot_count, dtype=jnp.int32)[:, None] == slot[None, :]
    offset_out = jnp.sum(jnp.where(in_slot, (query_pos % key_span + 1)[None, :], 0), axis=1) - 1
    slot_offset = exchange(offset_out.reshape(servers, capacity)).reshape(slot_count)
    pack = in_slot.astype(jnp.bfloat16)
    unpack = (slot[:, None] == jnp.arange(slot_count, dtype=jnp.int32)[None, :]).astype(jnp.bfloat16)
    tables = attend_tables(slot_offset, doc_blocks[0], heads)
    vt = jnp.swapaxes(pack_value_cache.reshape(key_span // KB, KB, HEAD_SIZE), 1, 2)

    queries = jnp.zeros((row_count, head_width), jnp.float32)
    for piece, shift, first in row_pieces(w_query):
        begin = member(me, shift) * depth + first
        left = lax.dynamic_slice_in_dim(hidden_rows, begin, piece.shape[0], 1)
        queries = queries + jnp.dot(left, piece, preferred_element_type=jnp.float32)
    outgoing = rounded(jnp.dot(pack, rounded(queries), preferred_element_type=jnp.float32))
    incoming = exchange(outgoing.reshape(servers, capacity, head_width)).reshape(slot_count, head_width)

    w_out, outgoing = lax.optimization_barrier((w_out, outgoing))
    out_pieces = row_pieces(w_out)

    attended = attend(incoming, tables, pack_key_cache, vt)
    returned = exchange(attended.reshape(servers, capacity, head_width)).reshape(slot_count, head_width)
    own_rows = rounded(jnp.dot(unpack, returned, preferred_element_type=jnp.float32))

    blocks = {}
    for piece, shift, first in out_pieces:
        term = jnp.dot(own_rows[:, first:first + piece.shape[0]], piece, preferred_element_type=jnp.float32)
        shift = (shift[0] % N_Y, *shift[1:])
        blocks[shift] = blocks[shift] + term if shift in blocks else term
    part = jnp.zeros((groups, row_count, servers * col_width // groups), jnp.bfloat16)
    for shift, term in blocks.items():
        who = member(me, shift)
        part = lax.dynamic_update_slice(
            part, rounded(term)[None], (who // N_CORE, jnp.int32(0), (who % N_CORE) * col_width)
        )
    return reduce_tensor(part)


def solution(mesh):
    return jax.shard_map(
        body,
        mesh=mesh,
        in_specs=(
            P("row", None),
            P("row", "tensor"),
            P("tensor", "row"),
            P("row", "tensor"),
            P("row", "tensor"),
            P("row"),
            P("row", None),
        ),
        out_specs=P("row", "tensor"),
        check_vma=False,
    )
```

```python
import functools
import math

import jax
import jax.numpy as jnp
from jax import lax
from jax.experimental import pallas as pl
from jax.experimental.pallas import tpu as pltpu
from jax.sharding import PartitionSpec as P


HEAD_SIZE = 128
NEG = -1e30
TILE = 64
KB = 1024
CHAIN = 128
N_Y, N_XH, N_CORE = 4, 2, 2
N_XL, N_Z = 2, 4
DEPTH = 512


def row_moves(to):
    at = lambda y, h, c: (y * N_XH + h) * N_CORE + c
    return [(at(y, h, c), at(*to(y, h, c))) for y in range(N_Y) for h in range(N_XH) for c in range(N_CORE)]


def tensor_moves(to):
    at = lambda xl, z: xl * N_Z + z
    return [(at(xl, z), at(*to(xl, z))) for xl in range(N_XL) for z in range(N_Z)]


Y_UP = row_moves(lambda y, h, c: ((y + 1) % N_Y, h, c))
Y_DOWN = row_moves(lambda y, h, c: ((y - 1) % N_Y, h, c))
H_FLIP = row_moves(lambda y, h, c: (y, 1 - h, c))
C_FLIP = row_moves(lambda y, h, c: (y, h, 1 - c))
Z_UP = tensor_moves(lambda xl, z: (xl, (z + 1) % N_Z))
Z_DOWN = tensor_moves(lambda xl, z: (xl, (z - 1) % N_Z))
XL_FLIP = tensor_moves(lambda xl, z: (1 - xl, z))
BOTH_FLIP = [(r * N_XL * N_Z + t, r2 * N_XL * N_Z + t2) for r, r2 in H_FLIP for t, t2 in XL_FLIP]


def over_row(x, moves):
    return lax.ppermute(x, "row", moves)


def over_tensor(x, moves):
    return lax.ppermute(x, "tensor", moves)


def with_other_core(pieces):
    out = []
    for piece, (dy, dh), first in pieces:
        out.append((piece, (dy % N_Y, dh, 0), first))
        out.append((over_row(piece, C_FLIP), (dy % N_Y, dh, 1), first))
    return out


def y_pieces(own, dh):
    half = own.shape[0] // 2
    up = over_row(own, Y_UP)
    down = over_row(own, Y_DOWN)
    up2 = over_row(up[:half], Y_UP)
    down2 = over_row(down[half:], Y_DOWN)
    return [(own, (0, dh), 0), (up, (-1, dh), 0), (down, (1, dh), 0), (up2, (-2, dh), 0), (down2, (2, dh), half)]


def far_hidden(hidden, h, z):
    rows, depth = hidden.shape
    width = depth // (N_Y * N_XH)
    mine = lax.dynamic_slice_in_dim(hidden, (z * N_XH + 1 - h) * width, width, 1)
    mine = lax.ppermute(mine, ("row", "tensor"), BOTH_FLIP)
    half = rows // 2
    up = over_tensor(mine, Z_UP)
    down = over_tensor(mine, Z_DOWN)
    up2 = over_tensor(up[:half], Z_UP)
    down2 = over_tensor(down[half:], Z_DOWN)
    return [(mine, 0, 0), (down, 1, 0), (up, 3, 0), (up2, 2, 0), (down2, 2, half)]


def far_kernel(lefts, rights, place, *refs):
    n_left, n_right = len(lefts), len(rights)
    left_in, right_in, out = refs[:n_left], refs[n_left:n_left + n_right], refs[n_left + n_right]
    stack, right_buf, sems = refs[-3], refs[-2], refs[-1]
    copies, at = [], 0
    for i, (step, first) in enumerate(lefts):
        rows = left_in[i].shape[0]
        copies.append(pltpu.make_async_copy(left_in[i], stack.at[step, pl.ds(first, rows), :], sems.at[i]))
    begins = []
    for i in range(n_right):
        rows = right_in[i].shape[0]
        copies.append(pltpu.make_async_copy(right_in[i], right_buf.at[pl.ds(at, rows), :], sems.at[n_left + i]))
        begins.append(at)
        at += rows
    for copy in copies:
        copy.start()
    for copy in copies[:n_left]:
        copy.wait()
    for i, ((dy, _, dc), first) in enumerate(rights):
        rows = right_in[i].shape[0]
        copies[n_left + i].wait()
        column = pl.multiple_of(lax.rem(place[1] + dc, N_CORE) * DEPTH + first, DEPTH // 2)
        left = stack[lax.rem(place[0] + dy, N_Y), :, pl.ds(column, rows)]
        term = jnp.dot(left, right_buf[begins[i]:begins[i] + rows, :], preferred_element_type=jnp.float32)
        if i == 0:
            out[...] = term
        else:
            out[...] += term


def far_product(lefts, rights, place):
    left_arrays, right_arrays = [p[0] for p in lefts], [p[0] for p in rights]
    rows, width = left_arrays[0].shape
    depth, columns = sum(a.shape[0] for a in right_arrays), right_arrays[0].shape[1]
    anywhere = [pl.BlockSpec(memory_space=pl.ANY)] * (len(lefts) + len(rights))
    return pl.pallas_call(
        functools.partial(far_kernel, [p[1:] for p in lefts], [p[1:] for p in rights]),
        out_shape=jax.ShapeDtypeStruct((rows, columns), jnp.float32),
        in_specs=[pl.BlockSpec(memory_space=pltpu.SMEM)] + anywhere,
        out_specs=pl.BlockSpec(memory_space=pltpu.VMEM),
        scratch_shapes=[
            pltpu.VMEM((N_Y, rows, width), jnp.bfloat16),
            pltpu.VMEM((depth, columns), jnp.bfloat16),
            pltpu.SemaphoreType.DMA((len(lefts) + len(rights),)),
        ],
        name="far_product",
    )(place, *left_arrays, *right_arrays)


def project_kernel(blocks, apart, place, rows, *refs):
    count = sum(len(parts) for _, parts in blocks)
    pieces, refs = refs[:count], refs[count:]
    if apart:
        mine, other, total_buf, refs = refs[0], refs[1], refs[-2], refs[2:-2] + refs[-1:]
    else:
        total_buf, refs = refs[0], refs[1:]
    bufs, sems = refs[:-1], refs[-1]
    copies = [pltpu.make_async_copy(pieces[i], bufs[i], sems.at[i]) for i in range(count)]
    for copy in copies:
        copy.start()
    width = pieces[0].shape[1]
    i = 0
    for (dy, dh, dc), firsts in blocks:
        total = None
        for first in firsts:
            copies[i].wait()
            depth = pieces[i].shape[0]
            term = jnp.dot(rows[:, first:first + depth], bufs[i][...], preferred_element_type=jnp.float32)
            total = term if total is None else total + term
            i += 1
        group = lax.rem(place[0] + dy, N_Y) * N_XH + lax.rem(place[1] + dh, N_XH)
        to_xl = lax.rem(group // N_Z + place[3], N_XL)
        to_z = lax.rem(lax.rem(group, N_Z) + N_Z - place[4], N_Z)
        begin = pl.multiple_of(lax.rem(place[2] + dc, N_CORE) * width, width)
        total_buf[to_z, to_xl, :, pl.ds(begin, width)] = total.astype(jnp.bfloat16)
    if apart:
        mine[...] = total_buf[:, 0]
        other[...] = total_buf[:, 1]


def project(rows, pieces, place, groups, apart):
    by_block = {}
    for piece, shift, first in pieces:
        by_block.setdefault(shift, []).append((first, piece))
    blocks = tuple((shift, tuple(first for first, _ in parts)) for shift, parts in by_block.items())
    arrays = [piece for parts in by_block.values() for _, piece in parts]
    count, width = rows.shape[0], len(blocks) * arrays[0].shape[1] // groups
    vmem = pl.BlockSpec(memory_space=pltpu.VMEM)
    whole = (N_Z, N_XL, count, width)
    one = jax.ShapeDtypeStruct((N_Z, count, width), jnp.bfloat16)
    return pl.pallas_call(
        functools.partial(project_kernel, blocks, apart),
        out_shape=(one, one) if apart else jax.ShapeDtypeStruct(whole, jnp.bfloat16),
        in_specs=[pl.BlockSpec(memory_space=pltpu.SMEM), vmem] + [pl.BlockSpec(memory_space=pl.ANY)] * len(arrays),
        out_specs=(vmem, vmem) if apart else vmem,
        scratch_shapes=[pltpu.VMEM(a.shape, a.dtype) for a in arrays]
        + ([pltpu.VMEM(whole, jnp.bfloat16)] if apart else [])
        + [pltpu.SemaphoreType.DMA((len(arrays),))],
    )(place, rows, *arrays)


def member(row, shift):
    dy, dh, dc = shift
    y, h, c = row // (N_XH * N_CORE), (row // N_CORE) % N_XH, row % N_CORE
    return (((y + dy) % N_Y) * N_XH + (h ^ dh)) * N_CORE + (c ^ dc)


def attend_kernel(heads, first_tile, last, bounds, perm, q, offs, starts, k, vt, *refs):
    if last:
        perm_t, before, out, sorted_q, sorted_o, acc = refs
    else:
        out, sorted_q, acc = refs
        sorted_o = out
    tiles = offs.shape[0]
    lanes = heads * TILE
    chains = range(lanes // CHAIN)
    sorted_q[...] = jnp.dot(perm[...], q[...], preferred_element_type=jnp.float32).astype(jnp.bfloat16)
    sorted_o[...] = jnp.zeros_like(sorted_o)
    scale = math.log2(math.e) / math.sqrt(HEAD_SIZE)

    def tile(t, carry):
        lo, hi = bounds[0, first_tile + t], bounds[1, first_tile + t]

        @pl.when(hi > lo)
        def _():
            rows = pl.ds(pl.multiple_of(t * TILE, TILE), TILE)
            qt = jnp.concatenate([sorted_q[rows, pl.ds(h * HEAD_SIZE, HEAD_SIZE)] for h in range(heads)], axis=0)
            parts = [qt[c * CHAIN:(c + 1) * CHAIN] for c in chains]
            acc[...] = jnp.zeros_like(acc)

            def block(b, state):
                kb = k[pl.ds(pl.multiple_of(b * KB, KB), KB), :]
                key = b * KB + lax.broadcasted_iota(jnp.int32, (KB, CHAIN), 0)
                bias = jnp.where((key <= offs[t, :, :CHAIN]) & (key >= starts[t, :, :CHAIN]), 0.0, NEG)
                scores = [
                    lax.dot_general(kb, part, (((1,), (1,)), ((), ())), preferred_element_type=jnp.float32)
                    for part in parts
                ]
                new = []
                for c in chains:
                    top, total = state[c]
                    s = scores[c] * scale + bias
                    new_top = jnp.maximum(top, jnp.max(s, axis=0, keepdims=True))
                    p = jnp.exp2(s - new_top)
                    alpha = jnp.exp2(top - new_top)
                    cols = pl.ds(c * CHAIN, CHAIN)
                    acc[:, cols] = acc[:, cols] * alpha + jnp.dot(
                        vt[b], p.astype(jnp.bfloat16), preferred_element_type=jnp.float32
                    )
                    new.append((new_top, total * alpha + jnp.sum(p, axis=0, keepdims=True)))
                return tuple(new)

            init = tuple(
                (jnp.full((1, CHAIN), NEG, jnp.float32), jnp.zeros((1, CHAIN), jnp.float32)) for _ in chains
            )
            final = lax.fori_loop(lo, hi, block, init)
            total = jnp.concatenate([state[1] for state in final], axis=1)
            o = (acc[...] * (1.0 / total)).T.astype(jnp.bfloat16)
            for h in range(heads):
                sorted_o[rows, pl.ds(h * HEAD_SIZE, HEAD_SIZE)] = o[h * TILE:(h + 1) * TILE]

        return carry

    lax.fori_loop(0, tiles, tile, 0)
    if last:
        rows = jnp.concatenate([before[...], sorted_o[...]], axis=0)
        out[...] = jnp.dot(perm_t[...], rows, preferred_element_type=jnp.float32).astype(jnp.bfloat16)


def attend_tables(slot_offset, doc_lengths, heads):
    slots = slot_offset.shape[0]
    tiles = slots // TILE
    key = jnp.where(slot_offset < 0, 1 << 20, slot_offset)
    idx = jnp.arange(slots, dtype=jnp.int32)
    before = (key[None, :] < key[:, None]) | ((key[None, :] == key[:, None]) & (idx[None, :] < idx[:, None]))
    rank = jnp.sum(before.astype(jnp.int32), axis=1)
    perm = rank[None, :] == idx[:, None]
    perm_t = rank[:, None] == idx[None, :]
    offset = jnp.sum(jnp.where(perm, slot_offset[None, :], 0), axis=1)
    start, end = jnp.zeros_like(offset), 0
    for d in range(doc_lengths.shape[0]):
        end = end + doc_lengths[d] * 128
        start = jnp.where(offset >= end, end, start)
    tile_offset, tile_start = offset.reshape(tiles, TILE), start.reshape(tiles, TILE)
    top = jnp.max(tile_offset, axis=1)
    lo = jnp.where(top >= 0, tile_start[:, 0] // KB, 0)
    hi = jnp.where(top >= 0, top // KB + 1, 0)

    def spread(a):
        return jnp.broadcast_to(a[:, None, :], (tiles, heads, TILE)).reshape(tiles, 1, heads * TILE)

    return (
        jnp.stack([lo, hi]),
        perm.astype(jnp.bfloat16),
        perm_t.astype(jnp.bfloat16),
        spread(tile_offset),
        spread(tile_start),
    )


def attend_run(q, tables, k, vt, before, first_tile, last_tile):
    slots, width = q.shape
    heads = width // HEAD_SIZE
    bounds, perm, perm_t, offs, starts = tables
    last = before is not None
    rows = (last_tile - first_tile) * TILE
    run = slice(first_tile, last_tile)
    perm = perm[first_tile * TILE:last_tile * TILE]
    arrays = [bounds, perm, q, offs[run], starts[run], k, vt] + ([perm_t, before] if last else [])
    vmem = pl.BlockSpec(memory_space=pltpu.VMEM)
    buffers = [pltpu.VMEM((rows, width), jnp.bfloat16)] * (2 if last else 1)
    return pl.pallas_call(
        functools.partial(attend_kernel, heads, first_tile, last),
        out_shape=jax.ShapeDtypeStruct((slots if last else rows, width), jnp.bfloat16),
        in_specs=[pl.BlockSpec(memory_space=pltpu.SMEM)] + [vmem] * (len(arrays) - 1),
        out_specs=vmem,
        scratch_shapes=buffers + [pltpu.VMEM((HEAD_SIZE, heads * TILE), jnp.float32)],
    )(*arrays)


def attend(q, tables, k, vt):
    tiles = q.shape[0] // TILE
    cut = (tiles * 5 + 7) // 8
    before = attend_run(q, tables, k, vt, None, 0, cut)
    return attend_run(q, tables, k, vt, before, cut, tiles)


def exchange(x):
    return lax.all_to_all(x, "row", split_axis=0, concat_axis=0, tiled=True)


def added(a, b):
    return a.astype(jnp.float32) + b.astype(jnp.float32)


def rounded(a):
    return a.astype(jnp.bfloat16)


def reduce_z(part):
    half = part.shape[2] // 2
    mine, up1, far, down1 = part[0], part[1], part[2], part[3]
    far_up = over_tensor(far[:, :half], Z_UP)
    far_down = over_tensor(far[:, half:], Z_DOWN)
    up_b = over_tensor(up1[:, half:], Z_UP)
    down_a = over_tensor(down1[:, :half], Z_DOWN)
    up_a = over_tensor(rounded(added(up1[:, :half], far_up)), Z_UP)
    down_b = over_tensor(rounded(added(down1[:, half:], far_down)), Z_DOWN)
    top = added(mine[:, :half], down_a) + up_a.astype(jnp.float32)
    low = added(mine[:, half:], up_b) + down_b.astype(jnp.float32)
    return jnp.concatenate([top, low], axis=1)


def sublayer(hidden_rows, w_query, w_out, pack_key_cache, pack_value_cache, query_pos, doc_blocks):
    servers = lax.axis_size("row")
    groups = lax.axis_size("tensor")
    me = lax.axis_index("row")
    row_count = hidden_rows.shape[0]
    key_span = pack_key_cache.shape[0]
    capacity = 2 * row_count // servers
    slot_count = servers * capacity
    depth, head_width = w_query.shape
    heads = head_width // HEAD_SIZE

    server = query_pos // key_span
    idx = jnp.arange(row_count, dtype=jnp.int32)
    earlier = (server[None, :] == server[:, None]) & (idx[None, :] < idx[:, None])
    slot = server * capacity + jnp.sum(earlier.astype(jnp.int32), axis=1)
    in_slot = jnp.arange(slot_count, dtype=jnp.int32)[:, None] == slot[None, :]
    offset_out = jnp.sum(jnp.where(in_slot, (query_pos % key_span + 1)[None, :], 0), axis=1) - 1
    slot_offset = exchange(offset_out.reshape(servers, capacity)).reshape(slot_count)
    pack = in_slot.astype(jnp.bfloat16)
    unpack = (slot[:, None] == jnp.arange(slot_count, dtype=jnp.int32)[None, :]).astype(jnp.bfloat16)

    y, h, core = me // (N_XH * N_CORE), (me // N_CORE) % N_XH, me % N_CORE
    z = lax.axis_index("tensor") % N_Z
    far = far_hidden(hidden_rows, h, z)
    query_pieces = with_other_core(y_pieces(w_query, 0))
    far_queries = far_product(far, query_pieces, jnp.stack([(y + N_Z - z) % N_Y, core]))
    hidden_rows, far_queries = lax.optimization_barrier((hidden_rows, far_queries))
    queries = jnp.zeros((row_count, head_width), jnp.float32)
    for piece, shift, first in query_pieces:
        left = lax.dynamic_slice_in_dim(hidden_rows, member(me, shift) * depth + first, piece.shape[0], 1)
        queries = queries + jnp.dot(left, piece, preferred_element_type=jnp.float32)
    queries = rounded(queries + over_row(far_queries, H_FLIP))
    outgoing = rounded(jnp.dot(pack, queries, preferred_element_type=jnp.float32))
    slot_offset, pack_value_cache, outgoing = lax.optimization_barrier((slot_offset, pack_value_cache, outgoing))
    incoming = exchange(outgoing.reshape(servers, capacity, head_width)).reshape(slot_count, head_width)
    tables = attend_tables(slot_offset, doc_blocks[0], heads)
    vt = jnp.swapaxes(pack_value_cache.reshape(key_span // KB, KB, HEAD_SIZE), 1, 2)

    other_h = over_row(w_out, H_FLIP)
    out_pieces = with_other_core(y_pieces(w_out, 0) + y_pieces(other_h, 1))

    attended = attend(incoming, tables, pack_key_cache, vt)
    returned = exchange(attended.reshape(servers, capacity, head_width)).reshape(slot_count, head_width)
    half = row_count // 2
    rows_of = lambda part: rounded(jnp.dot(part, returned, preferred_element_type=jnp.float32))
    t = lax.axis_index("tensor")
    place = jnp.stack([y, h, core, t // N_Z, z])
    mine, other = project(rows_of(unpack[half:]), out_pieces, place, groups, True)
    other = over_tensor(other, XL_FLIP)
    first = project(rows_of(unpack[:half]), out_pieces, place, groups, False)
    first = reduce_z(first)
    first = rounded(added(first[0], over_tensor(rounded(first[1]), XL_FLIP)))
    second = rounded(reduce_z(rounded(added(mine, other))[:, None])[0])
    return jnp.concatenate([first, second], axis=0)


def solution(mesh):
    return jax.shard_map(
        sublayer,
        mesh=mesh,
        in_specs=(
            P("row", None),
            P("row", "tensor"),
            P("tensor", "row"),
            P("row", "tensor"),
            P("row", "tensor"),
            P("row"),
            P("row", None),
        ),
        out_specs=P("row", "tensor"),
        check_vma=False,
    )
```

```python
import functools
import math

import jax
import jax.numpy as jnp
from jax import lax
from jax.experimental import pallas as pl
from jax.experimental.pallas import tpu as pltpu
from jax.sharding import PartitionSpec as P


HEAD_SIZE = 128
NEG = -1e30
TILE = 64
KB = 1024
CHAIN = 128
N_Y, N_XH, N_CORE = 4, 2, 2
N_XL, N_Z = 2, 4
DEPTH = 512


def row_moves(to):
    at = lambda y, h, c: (y * N_XH + h) * N_CORE + c
    return [(at(y, h, c), at(*to(y, h, c))) for y in range(N_Y) for h in range(N_XH) for c in range(N_CORE)]


def tensor_moves(to):
    at = lambda xl, z: xl * N_Z + z
    return [(at(xl, z), at(*to(xl, z))) for xl in range(N_XL) for z in range(N_Z)]


Y_UP = row_moves(lambda y, h, c: ((y + 1) % N_Y, h, c))
Y_DOWN = row_moves(lambda y, h, c: ((y - 1) % N_Y, h, c))
H_FLIP = row_moves(lambda y, h, c: (y, 1 - h, c))
C_FLIP = row_moves(lambda y, h, c: (y, h, 1 - c))
Z_UP = tensor_moves(lambda xl, z: (xl, (z + 1) % N_Z))
Z_DOWN = tensor_moves(lambda xl, z: (xl, (z - 1) % N_Z))
XL_FLIP = tensor_moves(lambda xl, z: (1 - xl, z))
BOTH_FLIP = [(r * N_XL * N_Z + t, r2 * N_XL * N_Z + t2) for r, r2 in H_FLIP for t, t2 in XL_FLIP]


def over_row(x, moves):
    return lax.ppermute(x, "row", moves)


def over_tensor(x, moves):
    return lax.ppermute(x, "tensor", moves)


def with_other_core(pieces):
    out = []
    for piece, (dy, dh), first in pieces:
        out.append((piece, (dy % N_Y, dh, 0), first))
        out.append((over_row(piece, C_FLIP), (dy % N_Y, dh, 1), first))
    return out


def y_pieces(own, dh):
    half = own.shape[0] // 2
    up = over_row(own, Y_UP)
    down = over_row(own, Y_DOWN)
    up2 = over_row(up[:half], Y_UP)
    down2 = over_row(down[half:], Y_DOWN)
    return [(own, (0, dh), 0), (up, (-1, dh), 0), (down, (1, dh), 0), (up2, (-2, dh), 0), (down2, (2, dh), half)]


def far_hidden(hidden, h, z):
    rows, depth = hidden.shape
    width = depth // (N_Y * N_XH)
    mine = lax.dynamic_slice_in_dim(hidden, (z * N_XH + 1 - h) * width, width, 1)
    mine = lax.ppermute(mine, ("row", "tensor"), BOTH_FLIP)
    half = rows // 2
    up = over_tensor(mine, Z_UP)
    down = over_tensor(mine, Z_DOWN)
    up2 = over_tensor(up[:half], Z_UP)
    down2 = over_tensor(down[half:], Z_DOWN)
    return [(mine, 0, 0), (down, 1, 0), (up, 3, 0), (up2, 2, 0), (down2, 2, half)]


def part_kernel(lefts, rights, place, *refs):
    n_left, n_right = max(len(lefts), 1), len(rights)
    left_in, right_in, out = refs[:n_left], refs[n_left:n_left + n_right], refs[n_left + n_right]
    stack, right_buf, sems = refs[-3], refs[-2], refs[-1]
    copies, at = [], 0
    for i, (step, first) in enumerate(lefts):
        rows = left_in[i].shape[0]
        copies.append(pltpu.make_async_copy(left_in[i], stack.at[step, pl.ds(first, rows), :], sems.at[i]))
    n_copies = len(lefts) or N_Y
    if not lefts:
        width = stack.shape[2]
        for step in range(N_Y):
            column = pl.multiple_of((step * N_XH + place[2]) * width, width)
            copies.append(pltpu.make_async_copy(left_in[0].at[:, pl.ds(column, width)], stack.at[step], sems.at[step]))
    begins = []
    for i in range(n_right):
        rows = right_in[i].shape[0]
        copies.append(pltpu.make_async_copy(right_in[i], right_buf.at[pl.ds(at, rows), :], sems.at[n_copies + i]))
        begins.append(at)
        at += rows
    for copy in copies:
        copy.start()
    for copy in copies[:n_copies]:
        copy.wait()
    for i, ((dy, _, dc), first) in enumerate(rights):
        rows = right_in[i].shape[0]
        copies[n_copies + i].wait()
        column = pl.multiple_of(lax.rem(place[1] + dc, N_CORE) * DEPTH + first, DEPTH // 2)
        left = stack[lax.rem(place[0] + dy, N_Y), :, pl.ds(column, rows)]
        term = jnp.dot(left, right_buf[begins[i]:begins[i] + rows, :], preferred_element_type=jnp.float32)
        if i == 0:
            out[...] = term
        else:
            out[...] += term


def part_product(lefts, rights, place, whole=None):
    left_arrays, right_arrays = [p[0] for p in lefts] or [whole], [p[0] for p in rights]
    rows, width = left_arrays[0].shape[0], DEPTH * N_CORE
    depth, columns = sum(a.shape[0] for a in right_arrays), right_arrays[0].shape[1]
    anywhere = [pl.BlockSpec(memory_space=pl.ANY)] * (len(left_arrays) + len(rights))
    return pl.pallas_call(
        functools.partial(part_kernel, [p[1:] for p in lefts], [p[1:] for p in rights]),
        out_shape=jax.ShapeDtypeStruct((rows, columns), jnp.float32),
        in_specs=[pl.BlockSpec(memory_space=pltpu.SMEM)]
        + anywhere,
        out_specs=pl.BlockSpec(memory_space=pltpu.VMEM),
        scratch_shapes=[
            pltpu.VMEM((N_Y, rows, width), jnp.bfloat16),
            pltpu.VMEM((depth, columns), jnp.bfloat16),
            pltpu.SemaphoreType.DMA(((len(lefts) or N_Y) + len(rights),)),
        ],
    )(place, *left_arrays, *right_arrays)


def project_kernel(blocks, apart, place, rows, *refs):
    count = sum(len(parts) for _, parts in blocks)
    pieces, refs = refs[:count], refs[count:]
    if apart:
        mine, other, total_buf, refs = refs[0], refs[1], refs[-2], refs[2:-2] + refs[-1:]
    else:
        total_buf, refs = refs[0], refs[1:]
    bufs, sems = refs[:-1], refs[-1]
    copies = [pltpu.make_async_copy(pieces[i], bufs[i], sems.at[i]) for i in range(count)]
    for copy in copies:
        copy.start()
    width = pieces[0].shape[1]
    i = 0
    for (dy, dh, dc), firsts in blocks:
        total = None
        for first in firsts:
            copies[i].wait()
            depth = pieces[i].shape[0]
            term = jnp.dot(rows[:, first:first + depth], bufs[i][...], preferred_element_type=jnp.float32)
            total = term if total is None else total + term
            i += 1
        group = lax.rem(place[0] + dy, N_Y) * N_XH + lax.rem(place[1] + dh, N_XH)
        to_xl = lax.rem(group // N_Z + place[3], N_XL)
        to_z = lax.rem(lax.rem(group, N_Z) + N_Z - place[4], N_Z)
        begin = pl.multiple_of(lax.rem(place[2] + dc, N_CORE) * width, width)
        total_buf[to_z, to_xl, :, pl.ds(begin, width)] = total.astype(jnp.bfloat16)
    if apart:
        mine[...] = total_buf[:, 0]
        other[...] = total_buf[:, 1]


def project(rows, pieces, place, groups, apart):
    by_block = {}
    for piece, shift, first in pieces:
        by_block.setdefault(shift, []).append((first, piece))
    blocks = tuple((shift, tuple(first for first, _ in parts)) for shift, parts in by_block.items())
    arrays = [piece for parts in by_block.values() for _, piece in parts]
    count, width = rows.shape[0], len(blocks) * arrays[0].shape[1] // groups
    vmem = pl.BlockSpec(memory_space=pltpu.VMEM)
    whole = (N_Z, N_XL, count, width)
    one = jax.ShapeDtypeStruct((N_Z, count, width), jnp.bfloat16)
    return pl.pallas_call(
        functools.partial(project_kernel, blocks, apart),
        out_shape=(one, one) if apart else jax.ShapeDtypeStruct(whole, jnp.bfloat16),
        in_specs=[pl.BlockSpec(memory_space=pltpu.SMEM), vmem] + [pl.BlockSpec(memory_space=pl.ANY)] * len(arrays),
        out_specs=(vmem, vmem) if apart else vmem,
        scratch_shapes=[pltpu.VMEM(a.shape, a.dtype) for a in arrays]
        + ([pltpu.VMEM(whole, jnp.bfloat16)] if apart else [])
        + [pltpu.SemaphoreType.DMA((len(arrays),))],
    )(place, rows, *arrays)


def attend_kernel(heads, first_tile, last, bounds, perm, q, offs, starts, k, vt, *refs):
    if last:
        perm_t, before, out, sorted_q, sorted_o, acc = refs
    else:
        out, sorted_q, acc = refs
        sorted_o = out
    tiles = offs.shape[0]
    lanes = heads * TILE
    chains = range(lanes // CHAIN)
    sorted_q[...] = jnp.dot(perm[...], q[...], preferred_element_type=jnp.float32).astype(jnp.bfloat16)
    sorted_o[...] = jnp.zeros_like(sorted_o)
    scale = math.log2(math.e) / math.sqrt(HEAD_SIZE)

    def tile(t, carry):
        lo, hi = bounds[0, first_tile + t], bounds[1, first_tile + t]

        @pl.when(hi > lo)
        def _():
            rows = pl.ds(pl.multiple_of(t * TILE, TILE), TILE)
            qt = jnp.concatenate([sorted_q[rows, pl.ds(h * HEAD_SIZE, HEAD_SIZE)] for h in range(heads)], axis=0)
            parts = [qt[c * CHAIN:(c + 1) * CHAIN] for c in chains]
            acc[...] = jnp.zeros_like(acc)

            def block(b, state):
                kb = k[pl.ds(pl.multiple_of(b * KB, KB), KB), :]
                key = b * KB + lax.broadcasted_iota(jnp.int32, (KB, CHAIN), 0)
                bias = jnp.where((key <= offs[t, :, :CHAIN]) & (key >= starts[t, :, :CHAIN]), 0.0, NEG)
                scores = [
                    lax.dot_general(kb, part, (((1,), (1,)), ((), ())), preferred_element_type=jnp.float32)
                    for part in parts
                ]
                new = []
                for c in chains:
                    top, total = state[c]
                    s = scores[c] * scale + bias
                    new_top = jnp.maximum(top, jnp.max(s, axis=0, keepdims=True))
                    p = jnp.exp2(s - new_top)
                    alpha = jnp.exp2(top - new_top)
                    cols = pl.ds(c * CHAIN, CHAIN)
                    acc[:, cols] = acc[:, cols] * alpha + jnp.dot(
                        vt[b], p.astype(jnp.bfloat16), preferred_element_type=jnp.float32
                    )
                    new.append((new_top, total * alpha + jnp.sum(p, axis=0, keepdims=True)))
                return tuple(new)

            init = tuple(
                (jnp.full((1, CHAIN), NEG, jnp.float32), jnp.zeros((1, CHAIN), jnp.float32)) for _ in chains
            )
            final = lax.fori_loop(lo, hi, block, init)
            total = jnp.concatenate([state[1] for state in final], axis=1)
            o = (acc[...] * (1.0 / total)).T.astype(jnp.bfloat16)
            for h in range(heads):
                sorted_o[rows, pl.ds(h * HEAD_SIZE, HEAD_SIZE)] = o[h * TILE:(h + 1) * TILE]

        return carry

    lax.fori_loop(0, tiles, tile, 0)
    if last:
        rows = jnp.concatenate([before[...], sorted_o[...]], axis=0)
        out[...] = jnp.dot(perm_t[...], rows, preferred_element_type=jnp.float32).astype(jnp.bfloat16)


def attend_tables(slot_offset, doc_lengths, heads):
    slots = slot_offset.shape[0]
    tiles = slots // TILE
    key = jnp.where(slot_offset < 0, 1 << 20, slot_offset)
    idx = jnp.arange(slots, dtype=jnp.int32)
    before = (key[None, :] < key[:, None]) | ((key[None, :] == key[:, None]) & (idx[None, :] < idx[:, None]))
    rank = jnp.sum(before.astype(jnp.int32), axis=1)
    perm = rank[None, :] == idx[:, None]
    perm_t = rank[:, None] == idx[None, :]
    offset = jnp.sum(jnp.where(perm, slot_offset[None, :], 0), axis=1)
    start, end = jnp.zeros_like(offset), 0
    for d in range(doc_lengths.shape[0]):
        end = end + doc_lengths[d] * 128
        start = jnp.where(offset >= end, end, start)
    tile_offset, tile_start = offset.reshape(tiles, TILE), start.reshape(tiles, TILE)
    top = jnp.max(tile_offset, axis=1)
    lo = jnp.where(top >= 0, tile_start[:, 0] // KB, 0)
    hi = jnp.where(top >= 0, top // KB + 1, 0)

    def spread(a):
        return jnp.broadcast_to(a[:, None, :], (tiles, heads, TILE)).reshape(tiles, 1, heads * TILE)

    return (
        jnp.stack([lo, hi]),
        perm.astype(jnp.bfloat16),
        perm_t.astype(jnp.bfloat16),
        spread(tile_offset),
        spread(tile_start),
    )


def attend_run(q, tables, k, vt, before, first_tile, last_tile):
    slots, width = q.shape
    heads = width // HEAD_SIZE
    bounds, perm, perm_t, offs, starts = tables
    last = before is not None
    rows = (last_tile - first_tile) * TILE
    run = slice(first_tile, last_tile)
    perm = perm[first_tile * TILE:last_tile * TILE]
    arrays = [bounds, perm, q, offs[run], starts[run], k, vt] + ([perm_t, before] if last else [])
    vmem = pl.BlockSpec(memory_space=pltpu.VMEM)
    buffers = [pltpu.VMEM((rows, width), jnp.bfloat16)] * (2 if last else 1)
    return pl.pallas_call(
        functools.partial(attend_kernel, heads, first_tile, last),
        out_shape=jax.ShapeDtypeStruct((slots if last else rows, width), jnp.bfloat16),
        in_specs=[pl.BlockSpec(memory_space=pltpu.SMEM)] + [vmem] * (len(arrays) - 1),
        out_specs=vmem,
        scratch_shapes=buffers + [pltpu.VMEM((HEAD_SIZE, heads * TILE), jnp.float32)],
    )(*arrays)


def attend(q, tables, k, vt):
    tiles = q.shape[0] // TILE
    cut = (tiles * 5 + 7) // 8
    before = attend_run(q, tables, k, vt, None, 0, cut)
    return attend_run(q, tables, k, vt, before, cut, tiles)


def exchange(x):
    return lax.all_to_all(x, "row", split_axis=0, concat_axis=0, tiled=True)


def added(a, b):
    return a.astype(jnp.float32) + b.astype(jnp.float32)


def rounded(a):
    return a.astype(jnp.bfloat16)


def reduce_z(part):
    half = part.shape[2] // 2
    mine, up1, far, down1 = part[0], part[1], part[2], part[3]
    far_up = over_tensor(far[:, :half], Z_UP)
    far_down = over_tensor(far[:, half:], Z_DOWN)
    up_b = over_tensor(up1[:, half:], Z_UP)
    down_a = over_tensor(down1[:, :half], Z_DOWN)
    up_a = over_tensor(rounded(added(up1[:, :half], far_up)), Z_UP)
    down_b = over_tensor(rounded(added(down1[:, half:], far_down)), Z_DOWN)
    top = added(mine[:, :half], down_a) + up_a.astype(jnp.float32)
    low = added(mine[:, half:], up_b) + down_b.astype(jnp.float32)
    return jnp.concatenate([top, low], axis=1)


def sublayer(hidden_rows, w_query, w_out, pack_key_cache, pack_value_cache, query_pos, doc_blocks):
    servers = lax.axis_size("row")
    groups = lax.axis_size("tensor")
    me = lax.axis_index("row")
    row_count = hidden_rows.shape[0]
    key_span = pack_key_cache.shape[0]
    capacity = 2 * row_count // servers
    slot_count = servers * capacity
    _, head_width = w_query.shape
    heads = head_width // HEAD_SIZE

    server = query_pos // key_span
    idx = jnp.arange(row_count, dtype=jnp.int32)
    earlier = (server[None, :] == server[:, None]) & (idx[None, :] < idx[:, None])
    slot = server * capacity + jnp.sum(earlier.astype(jnp.int32), axis=1)
    in_slot = jnp.arange(slot_count, dtype=jnp.int32)[:, None] == slot[None, :]
    offset_out = jnp.sum(jnp.where(in_slot, (query_pos % key_span + 1)[None, :], 0), axis=1) - 1
    slot_offset = exchange(offset_out.reshape(servers, capacity)).reshape(slot_count)
    pack = in_slot.astype(jnp.bfloat16)
    unpack = (slot[:, None] == jnp.arange(slot_count, dtype=jnp.int32)[None, :]).astype(jnp.bfloat16)

    y, h, core = me // (N_XH * N_CORE), (me // N_CORE) % N_XH, me % N_CORE
    z = lax.axis_index("tensor") % N_Z
    far = far_hidden(hidden_rows, h, z)
    query_pieces = with_other_core(y_pieces(w_query, 0))
    far_place = jnp.stack([(y + N_Z - z) % N_Y, core, h])
    far_queries = part_product(far, query_pieces, far_place)
    hidden_rows, far_queries = lax.optimization_barrier((hidden_rows, far_queries))
    queries = part_product([], query_pieces, jnp.stack([y, core, h]), whole=hidden_rows)
    queries = rounded(queries + over_row(far_queries, H_FLIP))
    outgoing = rounded(jnp.dot(pack, queries, preferred_element_type=jnp.float32))
    slot_offset, pack_value_cache, outgoing = lax.optimization_barrier((slot_offset, pack_value_cache, outgoing))
    incoming = exchange(outgoing.reshape(servers, capacity, head_width)).reshape(slot_count, head_width)
    tables = attend_tables(slot_offset, doc_blocks[0], heads)
    vt = jnp.swapaxes(pack_value_cache.reshape(key_span // KB, KB, HEAD_SIZE), 1, 2)

    other_h = over_row(w_out, H_FLIP)
    out_pieces = with_other_core(y_pieces(w_out, 0) + y_pieces(other_h, 1))

    attended = attend(incoming, tables, pack_key_cache, vt)
    returned = exchange(attended.reshape(servers, capacity, head_width)).reshape(slot_count, head_width)
    half = row_count // 2
    rows_of = lambda part: rounded(jnp.dot(part, returned, preferred_element_type=jnp.float32))
    t = lax.axis_index("tensor")
    place = jnp.stack([y, h, core, t // N_Z, z])
    mine, other = project(rows_of(unpack[half:]), out_pieces, place, groups, True)
    other = over_tensor(other, XL_FLIP)
    first = project(rows_of(unpack[:half]), out_pieces, place, groups, False)
    first = reduce_z(first)
    first = rounded(added(first[0], over_tensor(rounded(first[1]), XL_FLIP)))
    second = rounded(added(mine, other))
    second = rounded(reduce_z(second[:, None])[0])
    return jnp.concatenate([first, second], axis=0)


def solution(mesh):
    return jax.shard_map(
        sublayer,
        mesh=mesh,
        in_specs=(
            P("row", None),
            P("row", "tensor"),
            P("tensor", "row"),
            P("row", "tensor"),
            P("row", "tensor"),
            P("row"),
            P("row", None),
        ),
        out_specs=P("row", "tensor"),
        check_vma=False,
    )
```

```python
import functools
import math

import jax
import jax.numpy as jnp
from jax import lax
from jax.experimental import pallas as pl
from jax.experimental.pallas import tpu as pltpu
from jax.sharding import PartitionSpec as P


HEAD_SIZE = 128
NEG = -1e30
TILE = 64
KB = 1024
CHAIN = 128
N_Y, N_XH, N_CORE = 4, 2, 2
N_XL, N_Z = 2, 4
DEPTH = 512


def row_moves(to):
    at = lambda y, h, c: (y * N_XH + h) * N_CORE + c
    return [(at(y, h, c), at(*to(y, h, c))) for y in range(N_Y) for h in range(N_XH) for c in range(N_CORE)]


def tensor_moves(to):
    at = lambda xl, z: xl * N_Z + z
    return [(at(xl, z), at(*to(xl, z))) for xl in range(N_XL) for z in range(N_Z)]


Y_UP = row_moves(lambda y, h, c: ((y + 1) % N_Y, h, c))
Y_DOWN = row_moves(lambda y, h, c: ((y - 1) % N_Y, h, c))
H_FLIP = row_moves(lambda y, h, c: (y, 1 - h, c))
C_FLIP = row_moves(lambda y, h, c: (y, h, 1 - c))
Z_UP = tensor_moves(lambda xl, z: (xl, (z + 1) % N_Z))
Z_DOWN = tensor_moves(lambda xl, z: (xl, (z - 1) % N_Z))
XL_FLIP = tensor_moves(lambda xl, z: (1 - xl, z))
BOTH_FLIP = [(r * N_XL * N_Z + t, r2 * N_XL * N_Z + t2) for r, r2 in H_FLIP for t, t2 in XL_FLIP]


def over_row(x, moves):
    return lax.ppermute(x, "row", moves)


def over_tensor(x, moves):
    return lax.ppermute(x, "tensor", moves)


def with_other_core(pieces):
    out = []
    for piece, (dy, dh), first in pieces:
        out.append((piece, (dy % N_Y, dh, 0), first))
        out.append((over_row(piece, C_FLIP), (dy % N_Y, dh, 1), first))
    return out


def y_pieces(own, dh):
    half = own.shape[0] // 2
    up = over_row(own, Y_UP)
    down = over_row(own, Y_DOWN)
    up2 = over_row(up[:half], Y_UP)
    down2 = over_row(down[half:], Y_DOWN)
    return [(own, (0, dh), 0), (up, (-1, dh), 0), (down, (1, dh), 0), (up2, (-2, dh), 0), (down2, (2, dh), half)]


def far_hidden(hidden, h, z):
    rows, depth = hidden.shape
    width = depth // (N_Y * N_XH)
    mine = lax.dynamic_slice_in_dim(hidden, (z * N_XH + 1 - h) * width, width, 1)
    mine = lax.ppermute(mine, ("row", "tensor"), BOTH_FLIP)
    half = rows // 2
    up = over_tensor(mine, Z_UP)
    down = over_tensor(mine, Z_DOWN)
    up2 = over_tensor(up[:half], Z_UP)
    down2 = over_tensor(down[half:], Z_DOWN)
    return [(mine, 0, 0), (down, 1, 0), (up, 3, 0), (up2, 2, 0), (down2, 2, half)]


def part_kernel(lefts, rights, place, *refs):
    n_left, n_right = max(len(lefts), 1), len(rights)
    left_in, right_in, out = refs[:n_left], refs[n_left:n_left + n_right], refs[n_left + n_right]
    stack, right_buf, sems = refs[-3], refs[-2], refs[-1]
    copies, at = [], 0
    for i, (step, first) in enumerate(lefts):
        rows = left_in[i].shape[0]
        copies.append(pltpu.make_async_copy(left_in[i], stack.at[step, pl.ds(first, rows), :], sems.at[i]))
    n_copies = len(lefts) or N_Y
    if not lefts:
        width = stack.shape[2]
        for step in range(N_Y):
            column = pl.multiple_of((step * N_XH + place[2]) * width, width)
            copies.append(pltpu.make_async_copy(left_in[0].at[:, pl.ds(column, width)], stack.at[step], sems.at[step]))
    begins = []
    for i in range(n_right):
        rows = right_in[i].shape[0]
        copies.append(pltpu.make_async_copy(right_in[i], right_buf.at[pl.ds(at, rows), :], sems.at[n_copies + i]))
        begins.append(at)
        at += rows
    for copy in copies:
        copy.start()
    for copy in copies[:n_copies]:
        copy.wait()
    for i, ((dy, _, dc), first) in enumerate(rights):
        rows = right_in[i].shape[0]
        copies[n_copies + i].wait()
        column = pl.multiple_of(lax.rem(place[1] + dc, N_CORE) * DEPTH + first, DEPTH // 2)
        left = stack[lax.rem(place[0] + dy, N_Y), :, pl.ds(column, rows)]
        term = jnp.dot(left, right_buf[begins[i]:begins[i] + rows, :], preferred_element_type=jnp.float32)
        if i == 0:
            out[...] = term
        else:
            out[...] += term


def part_product(lefts, rights, place, whole=None):
    left_arrays, right_arrays = [p[0] for p in lefts] or [whole], [p[0] for p in rights]
    rows, width = left_arrays[0].shape[0], DEPTH * N_CORE
    depth, columns = sum(a.shape[0] for a in right_arrays), right_arrays[0].shape[1]
    anywhere = [pl.BlockSpec(memory_space=pl.ANY)] * (len(left_arrays) + len(rights))
    return pl.pallas_call(
        functools.partial(part_kernel, [p[1:] for p in lefts], [p[1:] for p in rights]),
        out_shape=jax.ShapeDtypeStruct((rows, columns), jnp.float32),
        in_specs=[pl.BlockSpec(memory_space=pltpu.SMEM)]
        + anywhere,
        out_specs=pl.BlockSpec(memory_space=pltpu.VMEM),
        scratch_shapes=[
            pltpu.VMEM((N_Y, rows, width), jnp.bfloat16),
            pltpu.VMEM((depth, columns), jnp.bfloat16),
            pltpu.SemaphoreType.DMA(((len(lefts) or N_Y) + len(rights),)),
        ],
    )(place, *left_arrays, *right_arrays)


def project_kernel(blocks, place, rows, *refs):
    count = sum(len(parts) for _, parts in blocks)
    pieces, (first_rows, mine, other), bufs, second_rows, sems = (
        refs[:count], refs[count:count + 3], refs[count + 3:-2], refs[-2], refs[-1]
    )
    copies = [pltpu.make_async_copy(pieces[i], bufs[i], sems.at[i]) for i in range(count)]
    for copy in copies:
        copy.start()
    width, half = pieces[0].shape[1], rows.shape[0] // 2
    i = 0
    for (dy, dh, dc), firsts in blocks:
        total = None
        for first in firsts:
            copies[i].wait()
            depth = pieces[i].shape[0]
            term = jnp.dot(rows[:, first:first + depth], bufs[i][...], preferred_element_type=jnp.float32)
            total = term if total is None else total + term
            i += 1
        total = total.astype(jnp.bfloat16)
        group = lax.rem(place[0] + dy, N_Y) * N_XH + lax.rem(place[1] + dh, N_XH)
        to_xl = lax.rem(group // N_Z + place[3], N_XL)
        to_z = lax.rem(lax.rem(group, N_Z) + N_Z - place[4], N_Z)
        begin = pl.multiple_of(lax.rem(place[2] + dc, N_CORE) * width, width)
        first_rows[to_z, to_xl, :, pl.ds(begin, width)] = total[:half]
        second_rows[to_z, to_xl, :, pl.ds(begin, width)] = total[half:]
    mine[...] = second_rows[:, 0]
    other[...] = second_rows[:, 1]


def project(rows, pieces, place, groups):
    by_block = {}
    for piece, shift, first in pieces:
        by_block.setdefault(shift, []).append((first, piece))
    blocks = tuple((shift, tuple(first for first, _ in parts)) for shift, parts in by_block.items())
    arrays = [piece for parts in by_block.values() for _, piece in parts]
    half, width = rows.shape[0] // 2, len(blocks) * arrays[0].shape[1] // groups
    vmem = pl.BlockSpec(memory_space=pltpu.VMEM)
    both = (N_Z, N_XL, half, width)
    one = jax.ShapeDtypeStruct((N_Z, half, width), jnp.bfloat16)
    return pl.pallas_call(
        functools.partial(project_kernel, blocks),
        out_shape=(jax.ShapeDtypeStruct(both, jnp.bfloat16), one, one),
        in_specs=[pl.BlockSpec(memory_space=pltpu.SMEM), vmem] + [pl.BlockSpec(memory_space=pl.ANY)] * len(arrays),
        out_specs=(vmem, vmem, vmem),
        scratch_shapes=[pltpu.VMEM(a.shape, a.dtype) for a in arrays]
        + [pltpu.VMEM(both, jnp.bfloat16), pltpu.SemaphoreType.DMA((len(arrays),))],
        name="project",
    )(place, rows, *arrays)


def attend_kernel(heads, first_tile, last, bounds, perm, q, offs, starts, k, vt, *refs):
    if last:
        perm_t, before, out, sorted_q, sorted_o, acc = refs
    else:
        out, sorted_q, acc = refs
        sorted_o = out
    tiles = offs.shape[0]
    lanes = heads * TILE
    chains = range(lanes // CHAIN)
    sorted_q[...] = jnp.dot(perm[...], q[...], preferred_element_type=jnp.float32).astype(jnp.bfloat16)
    sorted_o[...] = jnp.zeros_like(sorted_o)
    scale = math.log2(math.e) / math.sqrt(HEAD_SIZE)

    def tile(t, carry):
        lo, hi = bounds[0, first_tile + t], bounds[1, first_tile + t]

        @pl.when(hi > lo)
        def _():
            rows = pl.ds(pl.multiple_of(t * TILE, TILE), TILE)
            qt = jnp.concatenate([sorted_q[rows, pl.ds(h * HEAD_SIZE, HEAD_SIZE)] for h in range(heads)], axis=0)
            parts = [qt[c * CHAIN:(c + 1) * CHAIN] for c in chains]
            acc[...] = jnp.zeros_like(acc)

            def block(b, state):
                kb = k[pl.ds(pl.multiple_of(b * KB, KB), KB), :]
                key = b * KB + lax.broadcasted_iota(jnp.int32, (KB, CHAIN), 0)
                bias = jnp.where((key <= offs[t, :, :CHAIN]) & (key >= starts[t, :, :CHAIN]), 0.0, NEG)
                scores = [
                    lax.dot_general(kb, part, (((1,), (1,)), ((), ())), preferred_element_type=jnp.float32)
                    for part in parts
                ]
                new = []
                for c in chains:
                    top, total = state[c]
                    s = scores[c] * scale + bias
                    new_top = jnp.maximum(top, jnp.max(s, axis=0, keepdims=True))
                    p = jnp.exp2(s - new_top)
                    alpha = jnp.exp2(top - new_top)
                    cols = pl.ds(c * CHAIN, CHAIN)
                    acc[:, cols] = acc[:, cols] * alpha + jnp.dot(
                        vt[b], p.astype(jnp.bfloat16), preferred_element_type=jnp.float32
                    )
                    new.append((new_top, total * alpha + jnp.sum(p, axis=0, keepdims=True)))
                return tuple(new)

            init = tuple(
                (jnp.full((1, CHAIN), NEG, jnp.float32), jnp.zeros((1, CHAIN), jnp.float32)) for _ in chains
            )
            final = lax.fori_loop(lo, hi, block, init)
            total = jnp.concatenate([state[1] for state in final], axis=1)
            o = (acc[...] * (1.0 / total)).T.astype(jnp.bfloat16)
            for h in range(heads):
                sorted_o[rows, pl.ds(h * HEAD_SIZE, HEAD_SIZE)] = o[h * TILE:(h + 1) * TILE]

        return carry

    lax.fori_loop(0, tiles, tile, 0)
    if last:
        rows = jnp.concatenate([before[...], sorted_o[...]], axis=0)
        out[...] = jnp.dot(perm_t[...], rows, preferred_element_type=jnp.float32).astype(jnp.bfloat16)


def attend_tables(slot_offset, doc_lengths, heads):
    slots = slot_offset.shape[0]
    tiles = slots // TILE
    key = jnp.where(slot_offset < 0, 1 << 20, slot_offset)
    idx = jnp.arange(slots, dtype=jnp.int32)
    before = (key[None, :] < key[:, None]) | ((key[None, :] == key[:, None]) & (idx[None, :] < idx[:, None]))
    rank = jnp.sum(before.astype(jnp.int32), axis=1)
    perm = rank[None, :] == idx[:, None]
    perm_t = rank[:, None] == idx[None, :]
    offset = jnp.sum(jnp.where(perm, slot_offset[None, :], 0), axis=1)
    start, end = jnp.zeros_like(offset), 0
    for d in range(doc_lengths.shape[0]):
        end = end + doc_lengths[d] * 128
        start = jnp.where(offset >= end, end, start)
    tile_offset, tile_start = offset.reshape(tiles, TILE), start.reshape(tiles, TILE)
    top = jnp.max(tile_offset, axis=1)
    lo = jnp.where(top >= 0, tile_start[:, 0] // KB, 0)
    hi = jnp.where(top >= 0, top // KB + 1, 0)

    def spread(a):
        return jnp.broadcast_to(a[:, None, :], (tiles, heads, TILE)).reshape(tiles, 1, heads * TILE)

    return (
        jnp.stack([lo, hi]),
        perm.astype(jnp.bfloat16),
        perm_t.astype(jnp.bfloat16),
        spread(tile_offset),
        spread(tile_start),
    )


def attend_run(q, tables, k, vt, before, first_tile, last_tile):
    slots, width = q.shape
    heads = width // HEAD_SIZE
    bounds, perm, perm_t, offs, starts = tables
    last = before is not None
    rows = (last_tile - first_tile) * TILE
    run = slice(first_tile, last_tile)
    perm = perm[first_tile * TILE:last_tile * TILE]
    arrays = [bounds, perm, q, offs[run], starts[run], k, vt] + ([perm_t, before] if last else [])
    vmem = pl.BlockSpec(memory_space=pltpu.VMEM)
    buffers = [pltpu.VMEM((rows, width), jnp.bfloat16)] * (2 if last else 1)
    return pl.pallas_call(
        functools.partial(attend_kernel, heads, first_tile, last),
        out_shape=jax.ShapeDtypeStruct((slots if last else rows, width), jnp.bfloat16),
        in_specs=[pl.BlockSpec(memory_space=pltpu.SMEM)] + [vmem] * (len(arrays) - 1),
        out_specs=vmem,
        scratch_shapes=buffers + [pltpu.VMEM((HEAD_SIZE, heads * TILE), jnp.float32)],
    )(*arrays)


def attend(q, tables, k, vt):
    tiles = q.shape[0] // TILE
    cut = (tiles + 1) // 2
    before = attend_run(q, tables, k, vt, None, 0, cut)
    return attend_run(q, tables, k, vt, before, cut, tiles)


def exchange(x):
    return lax.all_to_all(x, "row", split_axis=0, concat_axis=0, tiled=True)


def added(a, b):
    return a.astype(jnp.float32) + b.astype(jnp.float32)


def rounded(a):
    return a.astype(jnp.bfloat16)


def reduce_z(part):
    half = part.shape[2] // 2
    mine, up1, far, down1 = part[0], part[1], part[2], part[3]
    far_up = over_tensor(far[:, :half], Z_UP)
    far_down = over_tensor(far[:, half:], Z_DOWN)
    up_b = over_tensor(up1[:, half:], Z_UP)
    down_a = over_tensor(down1[:, :half], Z_DOWN)
    up_a = over_tensor(rounded(added(up1[:, :half], far_up)), Z_UP)
    down_b = over_tensor(rounded(added(down1[:, half:], far_down)), Z_DOWN)
    top = added(mine[:, :half], down_a) + up_a.astype(jnp.float32)
    low = added(mine[:, half:], up_b) + down_b.astype(jnp.float32)
    return jnp.concatenate([top, low], axis=1)


def sublayer(hidden_rows, w_query, w_out, pack_key_cache, pack_value_cache, query_pos, doc_blocks):
    servers = lax.axis_size("row")
    groups = lax.axis_size("tensor")
    me = lax.axis_index("row")
    row_count = hidden_rows.shape[0]
    key_span = pack_key_cache.shape[0]
    capacity = 2 * row_count // servers
    slot_count = servers * capacity
    _, head_width = w_query.shape
    heads = head_width // HEAD_SIZE

    server = query_pos // key_span
    idx = jnp.arange(row_count, dtype=jnp.int32)
    earlier = (server[None, :] == server[:, None]) & (idx[None, :] < idx[:, None])
    slot = server * capacity + jnp.sum(earlier.astype(jnp.int32), axis=1)
    in_slot = jnp.arange(slot_count, dtype=jnp.int32)[:, None] == slot[None, :]
    offset_out = jnp.sum(jnp.where(in_slot, (query_pos % key_span + 1)[None, :], 0), axis=1) - 1
    slot_offset = exchange(offset_out.reshape(servers, capacity)).reshape(slot_count)
    pack = in_slot.astype(jnp.bfloat16)
    unpack = (slot[:, None] == jnp.arange(slot_count, dtype=jnp.int32)[None, :]).astype(jnp.bfloat16)

    y, h, core = me // (N_XH * N_CORE), (me // N_CORE) % N_XH, me % N_CORE
    z = lax.axis_index("tensor") % N_Z
    far = far_hidden(hidden_rows, h, z)
    query_pieces = with_other_core(y_pieces(w_query, 0))
    far_place = jnp.stack([(y + N_Z - z) % N_Y, core, h])
    far_queries = part_product(far, query_pieces, far_place)
    hidden_rows, far_queries = lax.optimization_barrier((hidden_rows, far_queries))
    queries = part_product([], query_pieces, jnp.stack([y, core, h]), whole=hidden_rows)
    queries = rounded(queries + over_row(far_queries, H_FLIP))
    outgoing = rounded(jnp.dot(pack, queries, preferred_element_type=jnp.float32))
    slot_offset, pack_value_cache, outgoing = lax.optimization_barrier((slot_offset, pack_value_cache, outgoing))
    incoming = exchange(outgoing.reshape(servers, capacity, head_width)).reshape(slot_count, head_width)
    tables = attend_tables(slot_offset, doc_blocks[0], heads)
    vt = jnp.swapaxes(pack_value_cache.reshape(key_span // KB, KB, HEAD_SIZE), 1, 2)

    other_h = over_row(w_out, H_FLIP)
    out_pieces = with_other_core(y_pieces(w_out, 0) + y_pieces(other_h, 1))

    attended = attend(incoming, tables, pack_key_cache, vt)
    returned = exchange(attended.reshape(servers, capacity, head_width)).reshape(slot_count, head_width)
    own_rows = rounded(jnp.dot(unpack, returned, preferred_element_type=jnp.float32))
    place = jnp.stack([y, h, core, lax.axis_index("tensor") // N_Z, z])
    first, mine, other = project(own_rows, out_pieces, place, groups)
    other = over_tensor(other, XL_FLIP)
    first = reduce_z(first)
    first = rounded(added(first[0], over_tensor(rounded(first[1]), XL_FLIP)))
    second = rounded(added(mine, other))
    second = rounded(reduce_z(second[:, None])[0])
    return jnp.concatenate([first, second], axis=0)


def solution(mesh):
    return jax.shard_map(
        sublayer,
        mesh=mesh,
        in_specs=(
            P("row", None),
            P("row", "tensor"),
            P("tensor", "row"),
            P("row", "tensor"),
            P("row", "tensor"),
            P("row"),
            P("row", None),
        ),
        out_specs=P("row", "tensor"),
        check_vma=False,
    )
```
